128 devices in a mesh: blk: 64 (over y_lo, x, z, core), feat: 2 (over y_hi).
Axes of the slice: x: 4, y: 4 (y_hi: 2, y_lo: 2; y = y_hi * 2 + y_lo), z: 4, core: 2. Of those that a mesh axis runs over, the one named last changes fastest.
Arguments:
- inputs: bfloat16 [131072, 128], P('blk'), may hold values from -6 to 6
- weight_h: bfloat16 [128, 128], P(None, 'feat'), may hold values from -0.5 to 0.5
- weight_s: bfloat16 [128, 4], replicated, may hold values from -0.75 to 0.75
- cotangent: bfloat16 [131072, 128], P('blk', 'feat'), may hold values from -6 to 6
- ranks: int32 [131072], P('blk'), may hold values from 0 to 2047, as said below
- counts: int32 [64], replicated, may hold values from 1024 to 2048, as said below
Outputs:
- grad_inputs: bfloat16 [131072, 128], P('blk', 'feat')
- grad_weight_h: float32 [128, 128], P(None, 'feat')
- grad_weight_s: float32 [128, 4], replicated
The draws below stay inside these ranges and needn't reach their ends.
Inputs may be any that keep to these rules, and one draw needn't show every extreme that they name: Within each block of 2048 hits the ranks are a permutation of 0 to 2047. `counts`: some block is full and some block holds exactly 1024 live hits.
All inputs are finite; a program needn't handle non-finite values.
Results may differ from the reference program's by a relative error of at most 0.0054.
Values may be sent and summed in bfloat16 or wider, within the bound.
No kernel may reach another device: no remote copies, remote signals or barrier semaphores. Data moves between devices by JAX's collectives and lax.ppermute only.
A program may use at most 128 MiB of HBM per device.

```python
import jax
import jax.numpy as jnp
from jax import lax

F = 128
DIN = 128
S = 4
WINDOW = 2
HITS_DEV = 2048
BLOCKS = 64
HITS = 131072


def draw_ranks(key, part):
    keys = jax.random.split(key, BLOCKS)
    return jax.vmap(lambda single: jax.random.permutation(single, HITS_DEV))(keys).reshape(-1).astype(jnp.int32)


def draw_counts(key, part):
    base = jax.random.randint(key, (BLOCKS,), HITS_DEV // 2, HITS_DEV + 1)
    order = jax.random.permutation(jax.random.fold_in(key, 7), BLOCKS)
    base = jnp.where(order == 0, HITS_DEV, base)
    base = jnp.where(order == 1, HITS_DEV // 2, base)
    return base.astype(jnp.int32)


def block_scale(rng, dims, cuts, smallest, top_value):
    level, own = 1.0, jax.random.fold_in(rng, 6)
    for position, parts in cuts:
        steps = jnp.exp(jax.random.uniform(jax.random.fold_in(own, position), (parts,), jnp.float32, smallest / len(cuts), top_value / len(cuts)))
        level = level * jnp.repeat(steps, dims[position] // parts).reshape([-1 if axis == position else 1 for axis in range(len(dims))])
    return level


def bell_draw(rng, dims, spread, limit, shards=(), kind=jnp.bfloat16):
    entries = spread * jax.random.normal(rng, dims, jnp.float32)
    if shards:
        entries = entries * block_scale(rng, dims, shards, -0.22, 0.18)
    return jnp.clip(entries, -limit, limit).astype(kind)


def setup_inputs(seed: int = 0) -> dict:
    streams_of = jax.random.split(jax.random.key(seed), 7)
    return {
        "inputs": bell_draw(streams_of[0], (HITS, DIN), 1.0, 6.0, ((0, 64),)),
        "weight_h": bell_draw(streams_of[1], (DIN, F), DIN ** -0.5, 0.5, ((1, 2),)),
        "weight_s": bell_draw(streams_of[2], (DIN, S), (DIN // 2) ** -0.5, 0.75),
        "cotangent": bell_draw(streams_of[3], (HITS, F), 1.0, 6.0, ((0, 64), (1, 2))),
        "ranks": draw_ranks(jax.random.fold_in(streams_of[6], 71), 0),
        "counts": draw_counts(jax.random.fold_in(streams_of[6], 71), 0),
    }


def reference(inputs, weight_h, weight_s, cotangent, ranks, counts):
    window = jnp.zeros((BLOCKS,), jnp.int32)
    for offset in range(-WINDOW, WINDOW + 1):
        window = window + jnp.roll(counts, -offset)
    live = (ranks.reshape(BLOCKS, HITS_DEV) < counts[:, None]).astype(jnp.float32)
    scale = 1.0 / jnp.sqrt(window.astype(jnp.float32))
    scaled = (cotangent.reshape(BLOCKS, HITS_DEV, F).astype(jnp.float32) * (live * scale[:, None])[:, :, None]).astype(jnp.bfloat16)
    masked = inputs * live.reshape(HITS, 1).astype(jnp.bfloat16)
    hidden = jnp.dot(masked, weight_h, preferred_element_type=jnp.float32).astype(jnp.bfloat16).reshape(BLOCKS, HITS_DEV, F)
    coords = jnp.dot(masked, weight_s, preferred_element_type=jnp.float32).reshape(BLOCKS, HITS_DEV, S).transpose(0, 2, 1)

    def one_block(index):
        scaled_a = scaled[index]
        hidden_a = hidden[index]
        coords_a = coords[index]
        hidden_sum = jnp.zeros((HITS_DEV, F), jnp.float32)
        coord_sum = jnp.zeros((S, HITS_DEV), jnp.float32)
        for offset in range(-WINDOW, WINDOW + 1):
            other = ((index + offset) % BLOCKS).astype(jnp.int32)
            scaled_b = scaled[other]
            hidden_b = hidden[other]
            coords_b = coords[other]
            square = jnp.zeros((HITS_DEV, HITS_DEV), jnp.float32)
            for component in range(S):
                square = square + (coords_a[component][:, None] - coords_b[component][None, :]) ** 2
            kernel = jnp.exp(-square)
            inner = jnp.dot(scaled_a, hidden_b.T, preferred_element_type=jnp.float32) + jnp.dot(hidden_a, scaled_b.T, preferred_element_type=jnp.float32)
            force = -kernel * inner
            hidden_sum = hidden_sum + jnp.dot(kernel.astype(jnp.bfloat16), scaled_b, preferred_element_type=jnp.float32)
            coord_sum = coord_sum + 2.0 * (coords_a * lax.optimization_barrier(jnp.sum(force, 1))[None, :] - jnp.dot(coords_b, force.T, precision=lax.Precision.HIGHEST))
        hidden_grad = (hidden_sum * live[index][:, None]).astype(jnp.bfloat16)
        return (hidden_grad, coord_sum)
    hidden_grad, coord_grad = lax.map(one_block, jnp.arange(BLOCKS, dtype=jnp.int32))
    hidden_flat = hidden_grad.reshape(HITS, F)
    coord_flat = coord_grad.transpose(0, 2, 1).reshape(HITS, S)
    grad_inputs = jnp.dot(hidden_flat, weight_h.T, preferred_element_type=jnp.float32) + jnp.dot(coord_flat, weight_s.astype(jnp.float32).T, precision=lax.Precision.HIGHEST)
    grad_weight_h = jnp.dot(masked.T, hidden_flat, preferred_element_type=jnp.float32)
    grad_weight_s = jnp.dot(masked.astype(jnp.float32).T, coord_flat, precision=lax.Precision.HIGHEST)
    return (grad_inputs.astype(jnp.bfloat16), grad_weight_h, grad_weight_s)
```

```python
import functools
import math

import jax
import jax.numpy as jnp
from jax import lax
from jax.experimental import pallas as pl
from jax.experimental.pallas import tpu as pltpu
from jax.sharding import PartitionSpec as P

WINDOW = 2
LOG2E = math.log2(math.e)
NT = (((1,), (1,)), ((), ()))
F32 = jnp.float32
BF16 = jnp.bfloat16
highest = lax.Precision.HIGHEST
ROW_TILE = 512
COL_TILE = 1024


def moved(x, target):
    blks, feats = lax.axis_size("blk"), lax.axis_size("feat")
    route = []
    for b in range(blks):
        for f in range(feats):
            to_b, to_f = target(b, f)
            route.append((b * feats + f, (to_b % blks) * feats + to_f))
    return lax.ppermute(x, ("blk", "feat"), route)


def split3(v):
    high = v.astype(BF16).astype(F32)
    rest = v - high
    mid = rest.astype(BF16).astype(F32)
    return high, mid, rest - mid


def norm_rows(v, row, first):
    parts = split3(-LOG2E * jnp.sum(v * v, axis=0, keepdims=True))
    out = jnp.where(row < 6, 1.0, 0.0)
    for i, part in enumerate(parts):
        out = jnp.where(row == first + i, part, out)
    return out


def far_features(coords):
    row = lax.broadcasted_iota(jnp.int32, coords.shape, 0)
    b1, b2, b3 = split3(coords)
    zero = jnp.zeros_like(coords)
    dist = jnp.concatenate([b1, b2, b3, b1, b2, b1, norm_rows(coords, row, 3), zero], 0)
    moment = jnp.concatenate([jnp.where(row == 4, 1.0, b1), b2, b3, zero], 0)
    return dist.astype(BF16), moment.astype(BF16)


def near_features(coords):
    row = lax.broadcasted_iota(jnp.int32, coords.shape, 0)
    a1, a2, a3 = split3((2.0 * LOG2E) * coords)
    zero = jnp.zeros_like(coords)
    dist = jnp.concatenate([a1, a1, a1, a2, a2, a3, norm_rows(coords, row, 0), zero], 0)
    return jnp.transpose(dist).astype(BF16)


def window_terms(near_dist, near_mix, mb, sb, w_t, ws_t, dist_sc, mix_sc, mom_sc, oh, oc, acc):
    dist, moment = far_features(
        lax.dot_general(ws_t[...], mb[...], NT, preferred_element_type=F32)
    )
    dist_sc[...] = dist
    mom_sc[...] = moment
    half = mix_sc.shape[0] // 2
    mix_sc[:half, :] = lax.dot_general(
        w_t[...], mb[...], NT, preferred_element_type=F32
    ).astype(BF16)
    mix_sc[half:, :] = sb[...]
    rows, cols = near_dist.shape[0], mb.shape[0]
    for r in range(0, rows, ROW_TILE):
        rs = slice(r, r + ROW_TILE)
        total_h = total_c = None
        if acc is not None:
            total_h, total_c = acc[0][rs, :], acc[1][rs, :]
        for c in range(0, cols, COL_TILE):
            cs = slice(c, c + COL_TILE)
            power = jnp.dot(near_dist[rs, :], dist_sc[:, cs], preferred_element_type=F32)
            inner = jnp.dot(near_mix[rs, :], mix_sc[:, cs], preferred_element_type=F32)
            kernel = jnp.exp2(power)
            force = (kernel * inner).astype(BF16)
            part_h = lax.dot_general(
                kernel.astype(BF16), sb[:, cs], NT, preferred_element_type=F32
            )
            part_c = lax.dot_general(force, mom_sc[:, cs], NT, preferred_element_type=F32)
            total_h = part_h if total_h is None else total_h + part_h
            total_c = part_c if total_c is None else total_c + part_c
        oh[rs, :] = total_h
        oc[rs, :] = total_c


def first_body(ma, sa, mb, sb, w, w_t, ws_t, oh, oc, near_dist, near_mix, dist_sc, mix_sc, mom_sc):
    near_dist[...] = near_features(
        lax.dot_general(ws_t[...], ma[...], NT, preferred_element_type=F32)
    )
    half = near_mix.shape[1] // 2
    near_mix[:, :half] = jnp.transpose(sa[...].astype(F32)).astype(BF16)
    near_mix[:, half:] = jnp.dot(ma[...], w[...], preferred_element_type=F32).astype(BF16)
    window_terms(near_dist, near_mix, mb, sb, w_t, ws_t, dist_sc, mix_sc, mom_sc, oh, oc, None)


def next_body(near_dist, near_mix, mb, sb, w_t, ws_t, ah, ac, oh, oc, dist_sc, mix_sc, mom_sc):
    window_terms(
        near_dist, near_mix, mb, sb, w_t, ws_t, dist_sc, mix_sc, mom_sc, oh, oc, (ah, ac)
    )


def call(body, operands, outs, cols, feats, **kw):
    vmem = pl.BlockSpec(memory_space=pltpu.VMEM)
    return pl.pallas_call(
        body,
        out_shape=outs,
        in_specs=[vmem] * len(operands),
        out_specs=[vmem] * len(outs),
        scratch_shapes=[
            pltpu.VMEM((64, cols), BF16),
            pltpu.VMEM((2 * feats, cols), BF16),
            pltpu.VMEM((32, cols), BF16),
        ],
        compiler_params=pltpu.CompilerParams(vmem_limit_bytes=48 << 20),
        **kw,
    )(*operands)


def local(inputs, weight_h, weight_s, cotangent, ranks, counts):
    block_total = lax.axis_size("blk")
    position = lax.axis_index("blk")
    my_half = lax.axis_index("feat")
    hits, width = cotangent.shape
    feats = 2 * width
    rows = hits // 2
    dims = weight_s.shape[1]
    blocks = jnp.arange(block_total, dtype=jnp.int32)
    spacing = (blocks - position) % block_total
    loop_gap = jnp.minimum(spacing, block_total - spacing)
    own_count = jnp.sum(jnp.where(blocks == position, counts, 0))
    window_count = jnp.sum(jnp.where(loop_gap <= WINDOW, counts, 0))
    live = (ranks < own_count).astype(F32)
    scale = 1.0 / jnp.sqrt(window_count.astype(F32))
    other_feat = lambda b, f: (b, 1 - f)

    masked = inputs * live.astype(BF16)[:, None]
    scaled_own = (cotangent.T.astype(F32) * (live * scale)[None, :]).astype(BF16)
    offsets = [1, -1, 2, -2][: 2 * WINDOW]
    masked_far = [moved(masked, lambda b, f, d=d: (b - d, f)) for d in offsets]
    scaled_other = moved(scaled_own, other_feat)
    w_own = weight_h
    w_other = moved(weight_h, other_feat)
    scaled = jnp.concatenate([scaled_own, scaled_other], 0)
    w = jnp.concatenate([w_own, w_other], 1)
    scaled_far = [moved(scaled, lambda b, f, d=d: (b - d, f)) for d in offsets]

    w_t = w.T
    ws_t = jnp.zeros((8, weight_s.shape[0]), BF16).at[:dims].set(weight_s.T)
    start = my_half * rows
    ma = lax.dynamic_slice_in_dim(masked, start, rows, 0)
    sa = lax.dynamic_slice_in_dim(scaled, start, rows, 1)
    sums = [
        jax.ShapeDtypeStruct((rows, feats), F32),
        jax.ShapeDtypeStruct((rows, 32), F32),
    ]
    near = [
        jax.ShapeDtypeStruct((rows, 64), BF16),
        jax.ShapeDtypeStruct((rows, 2 * feats), BF16),
    ]
    oh, oc, near_dist, near_mix = call(
        first_body, (ma, sa, masked, scaled, w, w_t, ws_t), sums + near, hits, feats
    )
    for mb, sb in zip(masked_far, scaled_far):
        oh, oc = call(
            next_body,
            (near_dist, near_mix, mb, sb, w_t, ws_t, oh, oc),
            sums,
            hits,
            feats,
            input_output_aliases={6: 0, 7: 1},
        )

    live_rows = lax.dynamic_slice_in_dim(live, start, rows, 0)
    hidden_grad = (oh * live_rows[:, None]).astype(BF16)
    coords = jnp.dot(ma, weight_s, preferred_element_type=F32)
    pulled = oc[:, :dims] + oc[:, 8 : 8 + dims] + oc[:, 16 : 16 + dims]
    coord_grad = 2.0 * (pulled - coords * oc[:, 4:5])
    part_h = lax.dot_general(
        hidden_grad, ma, (((0,), (0,)), ((), ())), preferred_element_type=F32
    )
    part_s = lax.dot_general(
        coord_grad, ma.astype(F32), (((0,), (0,)), ((), ())), precision=highest
    )
    total = jnp.concatenate([part_h[:width], part_s], 0) + moved(
        jnp.concatenate([part_h[width:], part_s], 0), other_feat
    )
    step = 1
    while step < block_total:
        total = total + moved(total, lambda b, f, s=step: (b ^ s, f))
        step *= 2
    grad_rows = lax.dot_general(hidden_grad, w, NT, preferred_element_type=F32) + jnp.dot(
        coord_grad, weight_s.astype(F32).T, precision=highest
    )
    grad_rows = grad_rows.astype(BF16)
    mine = lax.dynamic_slice_in_dim(grad_rows, my_half * width, width, 1)
    theirs = lax.dynamic_slice_in_dim(grad_rows, (1 - my_half) * width, width, 1)
    got = moved(theirs, other_feat)
    grad_inputs = jnp.where(
        my_half == 0, jnp.concatenate([mine, got], 0), jnp.concatenate([got, mine], 0)
    )
    return (grad_inputs, total[:width].T, total[width:].T)


def solution(mesh):
    placed = (P("blk", None), P(None, "feat"), P(), P("blk", "feat"), P("blk"), P())
    return jax.shard_map(
        local,
        mesh=mesh,
        in_specs=placed,
        out_specs=(P("blk", "feat"), P(None, "feat"), P()),
        check_vma=False,
    )
```

```python
import functools
import math

import jax
import jax.numpy as jnp
from jax import lax
from jax.experimental import pallas as pl
from jax.experimental.pallas import tpu as pltpu
from jax.sharding import PartitionSpec as P

WINDOW = 2
LOG2E = math.log2(math.e)
NT = (((1,), (1,)), ((), ()))
F32 = jnp.float32
BF16 = jnp.bfloat16
ROW_TILE = 512
COL_TILE = 1024


def moved(x, target):
    blks, feats = lax.axis_size("blk"), lax.axis_size("feat")
    route = []
    for b in range(blks):
        for f in range(feats):
            to_b, to_f = target(b, f)
            route.append((b * feats + f, (to_b % blks) * feats + to_f))
    return lax.ppermute(x, ("blk", "feat"), route)


def split3(v):
    high = v.astype(BF16).astype(F32)
    rest = v - high
    mid = rest.astype(BF16).astype(F32)
    return high, mid, rest - mid


def norm_rows(v, row, first):
    parts = split3(-LOG2E * jnp.sum(v * v, axis=0, keepdims=True))
    out = jnp.where(row < 6, 1.0, 0.0)
    for i, part in enumerate(parts):
        out = jnp.where(row == first + i, part, out)
    return out


def far_features(coords):
    row = lax.broadcasted_iota(jnp.int32, coords.shape, 0)
    b1, b2, b3 = split3(coords)
    zero = jnp.zeros_like(coords)
    dist = jnp.concatenate([b1, b2, b3, b1, b2, b1, norm_rows(coords, row, 3), zero], 0)
    moment = jnp.concatenate([jnp.where(row == 4, 1.0, b1), b2, b3, zero], 0)
    return dist.astype(BF16), moment.astype(BF16)


def near_features(coords):
    row = lax.broadcasted_iota(jnp.int32, coords.shape, 0)
    a1, a2, a3 = split3((2.0 * LOG2E) * coords)
    zero = jnp.zeros_like(coords)
    dist = jnp.concatenate([a1, a1, a1, a2, a2, a3, norm_rows(coords, row, 0), zero], 0)
    return jnp.transpose(dist).astype(BF16)


def window_terms(near_dist, near_mix, mb, sb, w_t, ws_t, dist_sc, mix_sc, mom_sc, oh, oc, acc):
    dist, moment = far_features(
        lax.dot_general(ws_t[...], mb[...], NT, preferred_element_type=F32)
    )
    dist_sc[...] = dist
    mom_sc[...] = moment
    half = mix_sc.shape[0] // 2
    mix_sc[:half, :] = lax.dot_general(
        w_t[...], mb[...], NT, preferred_element_type=F32
    ).astype(BF16)
    mix_sc[half:, :] = sb[...]
    rows, cols = near_dist.shape[0], mb.shape[0]
    for r in range(0, rows, ROW_TILE):
        rs = slice(r, r + ROW_TILE)
        total_h = total_c = None
        if acc is not None:
            total_h, total_c = acc[0][rs, :], acc[1][rs, :]
        for c in range(0, cols, COL_TILE):
            cs = slice(c, c + COL_TILE)
            power = jnp.dot(near_dist[rs, :], dist_sc[:, cs], preferred_element_type=F32)
            inner = jnp.dot(near_mix[rs, :], mix_sc[:, cs], preferred_element_type=F32)
            kernel = jnp.exp2(power)
            force = (kernel * inner).astype(BF16)
            part_h = lax.dot_general(
                kernel.astype(BF16), sb[:, cs], NT, preferred_element_type=F32
            )
            part_c = lax.dot_general(force, mom_sc[:, cs], NT, preferred_element_type=F32)
            total_h = part_h if total_h is None else total_h + part_h
            total_c = part_c if total_c is None else total_c + part_c
        oh[rs, :] = total_h
        oc[rs, :] = total_c


def first_body(ma, sa, mb, sb, w, w_t, ws_t, oh, oc, near_dist, near_mix, dist_sc, mix_sc, mom_sc):
    near_dist[...] = near_features(
        lax.dot_general(ws_t[...], ma[...], NT, preferred_element_type=F32)
    )
    half = near_mix.shape[1] // 2
    near_mix[:, :half] = jnp.transpose(sa[...].astype(F32)).astype(BF16)
    near_mix[:, half:] = jnp.dot(ma[...], w[...], preferred_element_type=F32).astype(BF16)
    window_terms(near_dist, near_mix, mb, sb, w_t, ws_t, dist_sc, mix_sc, mom_sc, oh, oc, None)


def next_body(near_dist, near_mix, mb, sb, w_t, ws_t, ah, ac, oh, oc, dist_sc, mix_sc, mom_sc):
    window_terms(
        near_dist, near_mix, mb, sb, w_t, ws_t, dist_sc, mix_sc, mom_sc, oh, oc, (ah, ac)
    )


def last_body(
    near_dist, near_mix, mb, sb, w_t, ws_t, ah, ac, ma, live, w_turned, ws_turned,
    own, other, mine, theirs, dist_sc, mix_sc, mom_sc, oh, oc,
):
    window_terms(
        near_dist, near_mix, mb, sb, w_t, ws_t, dist_sc, mix_sc, mom_sc, oh, oc, (ah, ac)
    )
    width = mine.shape[0]
    hidden_grad = (oh[...]).astype(BF16)
    sums = jnp.transpose(oc[...])
    coords = lax.dot_general(ws_t[...], ma[...], NT, preferred_element_type=F32)
    pulled = sums[0:8] + sums[8:16] + sums[16:24]
    coord_grad = 2.0 * (pulled - coords * sums[4:5])
    row = lax.broadcasted_iota(jnp.int32, coord_grad.shape, 0)
    coord_grad = jnp.where(row < 4, coord_grad, 0.0)
    g1, g2, g3 = split3(coord_grad)
    parts = jnp.concatenate([g1, g2, g3, jnp.zeros_like(g1)], 0).astype(BF16)
    part_h = lax.dot_general(
        hidden_grad, ma[...], (((0,), (0,)), ((), ())), preferred_element_type=F32
    )
    triple = jnp.dot(parts, ma[...], preferred_element_type=F32)
    part_s = triple[0:8] + triple[8:16] + triple[16:24]
    own[:width, :] = part_h[:width]
    own[width:, :] = part_s
    other[:width, :] = part_h[width:]
    other[width:, :] = part_s
    grad = lax.dot_general(w_turned[...], hidden_grad, NT, preferred_element_type=F32)
    grad = grad + jnp.dot(ws_turned[...], parts, preferred_element_type=F32)
    grad = (grad * live[...]).astype(BF16)
    mine[...] = grad[:width]
    theirs[...] = grad[width:]


def call(body, operands, outs, cols, feats, extra=(), **kw):
    vmem = pl.BlockSpec(memory_space=pltpu.VMEM)
    return pl.pallas_call(
        body,
        out_shape=outs,
        in_specs=[vmem] * len(operands),
        out_specs=[vmem] * len(outs),
        scratch_shapes=[
            pltpu.VMEM((64, cols), BF16),
            pltpu.VMEM((2 * feats, cols), BF16),
            pltpu.VMEM((32, cols), BF16),
            *extra,
        ],
        compiler_params=pltpu.CompilerParams(vmem_limit_bytes=48 << 20),
        **kw,
    )(*operands)


def local(inputs, weight_h, weight_s, cotangent, ranks, counts):
    block_total = lax.axis_size("blk")
    position = lax.axis_index("blk")
    my_half = lax.axis_index("feat")
    hits, width = cotangent.shape
    feats = 2 * width
    rows = hits // 2
    dims = weight_s.shape[1]
    blocks = jnp.arange(block_total, dtype=jnp.int32)
    spacing = (blocks - position) % block_total
    loop_gap = jnp.minimum(spacing, block_total - spacing)
    own_count = jnp.sum(jnp.where(blocks == position, counts, 0))
    window_count = jnp.sum(jnp.where(loop_gap <= WINDOW, counts, 0))
    live = (ranks < own_count).astype(F32)
    scale = 1.0 / jnp.sqrt(window_count.astype(F32))
    other_feat = lambda b, f: (b, 1 - f)

    packed = jnp.concatenate([cotangent.T, weight_h.T], 1)
    arrived = moved(packed, other_feat)
    masked = inputs * live.astype(BF16)[:, None]
    offsets = [1, -1, 2, -2][: 2 * WINDOW]
    masked_far = [moved(masked, lambda b, f, d=d: (b - d, f)) for d in offsets]
    both = jnp.concatenate([packed, arrived], 0)
    scaled = (both[:, :hits].astype(F32) * (live * scale)[None, :]).astype(BF16)
    w_t = both[:, hits:]
    w = w_t.T
    ws_t = jnp.zeros((8, weight_s.shape[0]), BF16).at[:dims].set(weight_s.T)
    turn = my_half * width
    w_turned = jnp.roll(w, -turn, 0)
    ws_turned = jnp.roll(
        jnp.concatenate([ws_t, ws_t, ws_t, jnp.zeros_like(ws_t)], 0).T, -turn, 0
    )
    start = my_half * rows
    ma = lax.dynamic_slice_in_dim(masked, start, rows, 0)
    sa = lax.dynamic_slice_in_dim(scaled, start, rows, 1)
    live_rows = lax.dynamic_slice_in_dim(live, start, rows, 0)[None, :]
    sums = [
        jax.ShapeDtypeStruct((rows, feats), F32),
        jax.ShapeDtypeStruct((rows, 32), F32),
    ]
    near = [
        jax.ShapeDtypeStruct((rows, 64), BF16),
        jax.ShapeDtypeStruct((rows, 2 * feats), BF16),
    ]
    scaled_far = [moved(scaled, lambda b, f, d=d: (b - d, f)) for d in offsets[:2]]
    oh, oc, near_dist, near_mix = call(
        first_body, (ma, sa, masked, scaled, w, w_t, ws_t), sums + near, hits, feats
    )
    late, oh, oc = lax.optimization_barrier((scaled, oh, oc))
    scaled_far += [moved(late, lambda b, f, d=d: (b - d, f)) for d in offsets[2:]]
    for mb, sb in list(zip(masked_far, scaled_far))[:-1]:
        oh, oc = call(
            next_body,
            (near_dist, near_mix, mb, sb, w_t, ws_t, oh, oc),
            sums,
            hits,
            feats,
            input_output_aliases={6: 0, 7: 1},
        )
    own, other, mine, theirs = call(
        last_body,
        (near_dist, near_mix, masked_far[-1], scaled_far[-1], w_t, ws_t, oh, oc)
        + (ma, live_rows, w_turned, ws_turned),
        [jax.ShapeDtypeStruct((width + 8, inputs.shape[1]), F32)] * 2
        + [jax.ShapeDtypeStruct((width, rows), BF16)] * 2,
        hits,
        feats,
        [pltpu.VMEM((rows, feats), F32), pltpu.VMEM((rows, 32), F32)],
    )
    total = own + moved(other, other_feat)
    step = 1
    while step < block_total:
        total = total + moved(total, lambda b, f, s=step: (b ^ s, f))
        step *= 2
    got = moved(theirs, other_feat)
    grad_inputs = jnp.where(
        my_half == 0, jnp.concatenate([mine, got], 1), jnp.concatenate([got, mine], 1)
    )
    return (grad_inputs.T, total[:width].T, total[width : width + dims].T)


def solution(mesh):
    placed = (P("blk", None), P(None, "feat"), P(), P("blk", "feat"), P("blk"), P())
    return jax.shard_map(
        local,
        mesh=mesh,
        in_specs=placed,
        out_specs=(P("blk", "feat"), P(None, "feat"), P()),
        check_vma=False,
    )
```

```python
import functools
import math

import jax
import jax.numpy as jnp
from jax import lax
from jax.experimental import pallas as pl
from jax.experimental.pallas import tpu as pltpu
from jax.sharding import PartitionSpec as P

WINDOW = 2
LOG2E = math.log2(math.e)
NT = (((1,), (1,)), ((), ()))
F32 = jnp.float32
BF16 = jnp.bfloat16
ROW_TILE = 512
COL_TILE = 1024


def moved(x, target):
    blks, feats = lax.axis_size("blk"), lax.axis_size("feat")
    route = []
    for b in range(blks):
        for f in range(feats):
            to_b, to_f = target(b, f)
            route.append((b * feats + f, (to_b % blks) * feats + to_f))
    return lax.ppermute(x, ("blk", "feat"), route)


def split3(v):
    high = v.astype(BF16).astype(F32)
    rest = v - high
    mid = rest.astype(BF16).astype(F32)
    return high, mid, rest - mid


def norm_rows(v, row, first):
    parts = split3(-LOG2E * jnp.sum(v * v, axis=0, keepdims=True))
    out = jnp.where(row < 6, 1.0, 0.0)
    for i, part in enumerate(parts):
        out = jnp.where(row == first + i, part, out)
    return out


def far_features(coords):
    row = lax.broadcasted_iota(jnp.int32, coords.shape, 0)
    b1, b2, b3 = split3(coords)
    zero = jnp.zeros_like(coords)
    dist = jnp.concatenate([b1, b2, b3, b1, b2, b1, norm_rows(coords, row, 3), zero], 0)
    moment = jnp.concatenate([jnp.where(row == 4, 1.0, b1), b2, b3, zero], 0)
    return dist.astype(BF16), moment.astype(BF16)


def near_features(coords):
    row = lax.broadcasted_iota(jnp.int32, coords.shape, 0)
    a1, a2, a3 = split3((2.0 * LOG2E) * coords)
    zero = jnp.zeros_like(coords)
    dist = jnp.concatenate([a1, a1, a1, a2, a2, a3, norm_rows(coords, row, 0), zero], 0)
    return jnp.transpose(dist).astype(BF16)


def window_terms(near_dist, near_mix, mb, sb, w_t, ws_t, dist_sc, mix_sc, mom_sc, oh, oc, acc):
    dist, moment = far_features(
        lax.dot_general(ws_t[...], mb[...], NT, preferred_element_type=F32)
    )
    dist_sc[...] = dist
    mom_sc[...] = moment
    half = mix_sc.shape[0] // 2
    mix_sc[:half, :] = lax.dot_general(
        w_t[...], mb[...], NT, preferred_element_type=F32
    ).astype(BF16)
    mix_sc[half:, :] = sb[...]
    rows, cols = near_dist.shape[0], mb.shape[0]
    for r in range(0, rows, ROW_TILE):
        rs = slice(r, r + ROW_TILE)
        total_h = total_c = None
        if acc is not None:
            total_h, total_c = acc[0][rs, :], acc[1][rs, :]
        for c in range(0, cols, COL_TILE):
            cs = slice(c, c + COL_TILE)
            power = jnp.dot(near_dist[rs, :], dist_sc[:, cs], preferred_element_type=F32)
            inner = jnp.dot(near_mix[rs, :], mix_sc[:, cs], preferred_element_type=F32)
            kernel = jnp.exp2(power)
            force = (kernel * inner).astype(BF16)
            part_h = lax.dot_general(
                kernel.astype(BF16), sb[:, cs], NT, preferred_element_type=F32
            )
            part_c = lax.dot_general(force, mom_sc[:, cs], NT, preferred_element_type=F32)
            total_h = part_h if total_h is None else total_h + part_h
            total_c = part_c if total_c is None else total_c + part_c
        oh[rs, :] = total_h
        oc[rs, :] = total_c


def first_body(ma, sa, mb, sb, w, w_t, ws_t, oh, oc, near_dist, near_mix, dist_sc, mix_sc, mom_sc):
    near_dist[...] = near_features(
        lax.dot_general(ws_t[...], ma[...], NT, preferred_element_type=F32)
    )
    half = near_mix.shape[1] // 2
    near_mix[:, :half] = jnp.transpose(sa[...].astype(F32)).astype(BF16)
    near_mix[:, half:] = jnp.dot(ma[...], w[...], preferred_element_type=F32).astype(BF16)
    window_terms(near_dist, near_mix, mb, sb, w_t, ws_t, dist_sc, mix_sc, mom_sc, oh, oc, None)


def next_body(near_dist, near_mix, mb, sb, w_t, ws_t, ah, ac, oh, oc, dist_sc, mix_sc, mom_sc):
    window_terms(
        near_dist, near_mix, mb, sb, w_t, ws_t, dist_sc, mix_sc, mom_sc, oh, oc, (ah, ac)
    )


def pack_body(cot_t, wh_t, out):
    hits = cot_t.shape[1]
    out[:, :hits] = cot_t[...]
    out[:, hits:] = wh_t[...]


def spread_body(half, packed, arrived, factor, ws_t, scaled, sa, w, w_t, w_turned, ws_turned):
    width = packed.shape[0]
    hits, rows = factor.shape[1], sa.shape[1]
    for i, ref in enumerate((packed, arrived)):
        rs = slice(i * width, (i + 1) * width)
        value = (ref[:, :hits].astype(F32) * factor[...]).astype(BF16)
        scaled[rs, :] = value
        w_t[rs, :] = ref[:, hits:]

        @pl.when(half[0] == 0)
        def _():
            sa[rs, :] = value[:, :rows]

        @pl.when(half[0] == 1)
        def _():
            sa[rs, :] = value[:, rows:]

    full = jnp.transpose(w_t[...].astype(F32))
    w[...] = full.astype(BF16)
    triple = jnp.concatenate([ws_t[...].astype(F32)] * 3 + [jnp.zeros(ws_t.shape, F32)], 0)
    sides = jnp.transpose(triple)

    @pl.when(half[0] == 0)
    def _():
        w_turned[...] = full.astype(BF16)
        ws_turned[...] = sides.astype(BF16)

    @pl.when(half[0] == 1)
    def _():
        w_turned[...] = jnp.concatenate([full[width:], full[:width]], 0).astype(BF16)
        ws_turned[...] = jnp.concatenate([sides[width:], sides[:width]], 0).astype(BF16)


def last_body(
    near_dist, near_mix, mb, sb, w_t, ws_t, ah, ac, ma, live, w_turned, ws_turned,
    own, other, mine, theirs, dist_sc, mix_sc, mom_sc, oh, oc,
):
    window_terms(
        near_dist, near_mix, mb, sb, w_t, ws_t, dist_sc, mix_sc, mom_sc, oh, oc, (ah, ac)
    )
    width = mine.shape[0]
    hidden_grad = (oh[...]).astype(BF16)
    sums = jnp.transpose(oc[...])
    coords = lax.dot_general(ws_t[...], ma[...], NT, preferred_element_type=F32)
    pulled = sums[0:8] + sums[8:16] + sums[16:24]
    coord_grad = 2.0 * (pulled - coords * sums[4:5])
    row = lax.broadcasted_iota(jnp.int32, coord_grad.shape, 0)
    coord_grad = jnp.where(row < 4, coord_grad, 0.0)
    g1, g2, g3 = split3(coord_grad)
    parts = jnp.concatenate([g1, g2, g3, jnp.zeros_like(g1)], 0).astype(BF16)
    part_h = lax.dot_general(
        hidden_grad, ma[...], (((0,), (0,)), ((), ())), preferred_element_type=F32
    )
    triple = jnp.dot(parts, ma[...], preferred_element_type=F32)
    part_s = triple[0:8] + triple[8:16] + triple[16:24]
    own[:width, :] = part_h[:width]
    own[width:, :] = part_s
    other[:width, :] = part_h[width:]
    other[width:, :] = part_s
    grad = lax.dot_general(w_turned[...], hidden_grad, NT, preferred_element_type=F32)
    grad = grad + jnp.dot(ws_turned[...], parts, preferred_element_type=F32)
    grad = (grad * live[...]).astype(BF16)
    mine[...] = grad[:width]
    theirs[...] = grad[width:]


def call(body, operands, outs, cols, feats, extra=(), **kw):
    vmem = pl.BlockSpec(memory_space=pltpu.VMEM)
    return pl.pallas_call(
        body,
        out_shape=outs,
        in_specs=[vmem] * len(operands),
        out_specs=[vmem] * len(outs),
        scratch_shapes=[
            pltpu.VMEM((64, cols), BF16),
            pltpu.VMEM((2 * feats, cols), BF16),
            pltpu.VMEM((32, cols), BF16),
            *extra,
        ],
        compiler_params=pltpu.CompilerParams(vmem_limit_bytes=48 << 20),
        cost_estimate=pl.CostEstimate(
            flops=4 * cols * cols * feats, transcendentals=cols * cols // 2, bytes_accessed=4 * cols * feats
        ),
        **kw,
    )(*operands)


def local(inputs, weight_h, weight_s, cotangent, ranks, counts):
    block_total = lax.axis_size("blk")
    position = lax.axis_index("blk")
    my_half = lax.axis_index("feat")
    hits, width = cotangent.shape
    feats = 2 * width
    rows = hits // 2
    dims = weight_s.shape[1]
    blocks = jnp.arange(block_total, dtype=jnp.int32)
    spacing = (blocks - position) % block_total
    loop_gap = jnp.minimum(spacing, block_total - spacing)
    own_count = jnp.sum(jnp.where(blocks == position, counts, 0))
    window_count = jnp.sum(jnp.where(loop_gap <= WINDOW, counts, 0))
    live = (ranks < own_count).astype(F32)
    scale = 1.0 / jnp.sqrt(window_count.astype(F32))
    other_feat = lambda b, f: (b, 1 - f)

    vmem = pl.BlockSpec(memory_space=pltpu.VMEM)
    depth = inputs.shape[1]
    packed = pl.pallas_call(
        pack_body,
        out_shape=jax.ShapeDtypeStruct((width, hits + depth), BF16),
        in_specs=[vmem] * 2,
        out_specs=vmem,
    )(cotangent.T, weight_h.T)
    arrived = moved(packed, other_feat)
    masked = inputs * live.astype(BF16)[:, None]
    offsets = [1, -1, 2, -2][: 2 * WINDOW]
    masked_far = [moved(masked, lambda b, f, d=d: (b - d, f)) for d in offsets]
    ws_t = jnp.zeros((8, depth), BF16).at[:dims].set(weight_s.T)
    shapes = [(feats, hits), (feats, rows), (depth, feats), (feats, depth), (depth, feats)]
    scaled, sa, w, w_t, w_turned, ws_turned = pl.pallas_call(
        spread_body,
        out_shape=[jax.ShapeDtypeStruct(shape, BF16) for shape in shapes + [(depth, 32)]],
        in_specs=[pl.BlockSpec(memory_space=pltpu.SMEM)] + [vmem] * 4,
        out_specs=[vmem] * 6,
        compiler_params=pltpu.CompilerParams(vmem_limit_bytes=32 << 20),
    )(my_half[None], packed, arrived, (live * scale)[None, :], ws_t)
    start = my_half * rows
    ma = lax.dynamic_slice_in_dim(masked, start, rows, 0)
    live_rows = lax.dynamic_slice_in_dim(live, start, rows, 0)[None, :]
    sums = [
        jax.ShapeDtypeStruct((rows, feats), F32),
        jax.ShapeDtypeStruct((rows, 32), F32),
    ]
    near = [
        jax.ShapeDtypeStruct((rows, 64), BF16),
        jax.ShapeDtypeStruct((rows, 2 * feats), BF16),
    ]
    scaled_far = [moved(scaled, lambda b, f, d=d: (b - d, f)) for d in offsets]
    oh, oc, near_dist, near_mix = call(
        first_body, (ma, sa, masked, scaled, w, w_t, ws_t), sums + near, hits, feats
    )
    for mb, sb in list(zip(masked_far, scaled_far))[:-1]:
        oh, oc = call(
            next_body,
            (near_dist, near_mix, mb, sb, w_t, ws_t, oh, oc),
            sums,
            hits,
            feats,
            input_output_aliases={6: 0, 7: 1},
        )
    own, other, mine, theirs = call(
        last_body,
        (near_dist, near_mix, masked_far[-1], scaled_far[-1], w_t, ws_t, oh, oc)
        + (ma, live_rows, w_turned, ws_turned),
        [jax.ShapeDtypeStruct((width + 8, inputs.shape[1]), F32)] * 2
        + [jax.ShapeDtypeStruct((width, rows), BF16)] * 2,
        hits,
        feats,
        [pltpu.VMEM((rows, feats), F32), pltpu.VMEM((rows, 32), F32)],
    )
    total = own + moved(other, other_feat)
    step = 1
    while step < block_total:
        total = total + moved(total, lambda b, f, s=step: (b ^ s, f))
        step *= 2
    got = moved(theirs, other_feat)
    grad_inputs = jnp.where(
        my_half == 0, jnp.concatenate([mine, got], 1), jnp.concatenate([got, mine], 1)
    )
    return (grad_inputs.T, total[:width].T, total[width : width + dims].T)


def solution(mesh):
    placed = (P("blk", None), P(None, "feat"), P(), P("blk", "feat"), P("blk"), P())
    return jax.shard_map(
        local,
        mesh=mesh,
        in_specs=placed,
        out_specs=(P("blk", "feat"), P(None, "feat"), P()),
        check_vma=False,
    )
```

```python
import functools
import math

import jax
import jax.numpy as jnp
from jax import lax
from jax.experimental import pallas as pl
from jax.experimental.pallas import tpu as pltpu
from jax.sharding import PartitionSpec as P

WINDOW = 2
LOG2E = math.log2(math.e)
NT = (((1,), (1,)), ((), ()))
F32 = jnp.float32
BF16 = jnp.bfloat16
ROW_TILE = 512
COL_TILE = 1024


def moved(x, target):
    blks, feats = lax.axis_size("blk"), lax.axis_size("feat")
    route = []
    for b in range(blks):
        for f in range(feats):
            to_b, to_f = target(b, f)
            route.append((b * feats + f, (to_b % blks) * feats + to_f))
    return lax.ppermute(x, ("blk", "feat"), route)


def split3(v):
    high = v.astype(BF16).astype(F32)
    rest = v - high
    mid = rest.astype(BF16).astype(F32)
    return high, mid, rest - mid


def norm_rows(v, row, first):
    parts = split3(-LOG2E * jnp.sum(v * v, axis=0, keepdims=True))
    out = jnp.where(row < 6, 1.0, 0.0)
    for i, part in enumerate(parts):
        out = jnp.where(row == first + i, part, out)
    return out


def far_features(coords):
    row = lax.broadcasted_iota(jnp.int32, coords.shape, 0)
    b1, b2, b3 = split3(coords)
    zero = jnp.zeros_like(coords)
    dist = jnp.concatenate([b1, b2, b3, b1, b2, b1, norm_rows(coords, row, 3), zero], 0)
    moment = jnp.concatenate([jnp.where(row == 4, 1.0, b1), b2, b3, zero], 0)
    return dist.astype(BF16), moment.astype(BF16)


def near_features(coords):
    row = lax.broadcasted_iota(jnp.int32, coords.shape, 0)
    a1, a2, a3 = split3((2.0 * LOG2E) * coords)
    zero = jnp.zeros_like(coords)
    dist = jnp.concatenate([a1, a1, a1, a2, a2, a3, norm_rows(coords, row, 0), zero], 0)
    return jnp.transpose(dist).astype(BF16)


def window_terms(near_dist, near_mix, mb, sb, w_t, ws_t, dist_sc, mix_sc, mom_sc, oh, oc, acc):
    dist, moment = far_features(
        lax.dot_general(ws_t[...], mb[...], NT, preferred_element_type=F32)
    )
    dist_sc[...] = dist
    mom_sc[...] = moment
    half = mix_sc.shape[0] // 2
    mix_sc[:half, :] = lax.dot_general(
        w_t[...], mb[...], NT, preferred_element_type=F32
    ).astype(BF16)
    mix_sc[half:, :] = sb[...]
    rows, cols = near_dist.shape[0], mb.shape[0]
    for r in range(0, rows, ROW_TILE):
        rs = slice(r, r + ROW_TILE)
        total_h = total_c = None
        if acc is not None:
            total_h, total_c = acc[0][rs, :], acc[1][rs, :]
        for c in range(0, cols, COL_TILE):
            cs = slice(c, c + COL_TILE)
            power = jnp.dot(near_dist[rs, :], dist_sc[:, cs], preferred_element_type=F32)
            inner = jnp.dot(near_mix[rs, :], mix_sc[:, cs], preferred_element_type=F32)
            kernel = jnp.exp2(power)
            force = (kernel * inner).astype(BF16)
            part_h = lax.dot_general(
                kernel.astype(BF16), sb[:, cs], NT, preferred_element_type=F32
            )
            part_c = lax.dot_general(force, mom_sc[:, cs], NT, preferred_element_type=F32)
            total_h = part_h if total_h is None else total_h + part_h
            total_c = part_c if total_c is None else total_c + part_c
        oh[rs, :] = total_h
        oc[rs, :] = total_c


def first_body(ma, sa, mb, sb, w, w_t, ws_t, oh, oc, near_dist, near_mix, dist_sc, mix_sc, mom_sc):
    near_dist[...] = near_features(
        lax.dot_general(ws_t[...], ma[...], NT, preferred_element_type=F32)
    )
    half = near_mix.shape[1] // 2
    near_mix[:, :half] = jnp.transpose(sa[...].astype(F32)).astype(BF16)
    near_mix[:, half:] = jnp.dot(ma[...], w[...], preferred_element_type=F32).astype(BF16)
    window_terms(near_dist, near_mix, mb, sb, w_t, ws_t, dist_sc, mix_sc, mom_sc, oh, oc, None)


def next_body(near_dist, near_mix, mb, sb, w_t, ws_t, ah, ac, oh, oc, dist_sc, mix_sc, mom_sc):
    window_terms(
        near_dist, near_mix, mb, sb, w_t, ws_t, dist_sc, mix_sc, mom_sc, oh, oc, (ah, ac)
    )


def pack_body(cot_t, wh_t, out):
    hits = cot_t.shape[1]
    out[:, :hits] = cot_t[...]
    out[:, hits:] = wh_t[...]


def spread_body(half, packed, arrived, factor, ws_t, scaled, sa, w, w_t, w_turned, ws_turned):
    width = packed.shape[0]
    hits, rows = factor.shape[1], sa.shape[1]
    for i, ref in enumerate((packed, arrived)):
        rs = slice(i * width, (i + 1) * width)
        value = (ref[:, :hits].astype(F32) * factor[...]).astype(BF16)
        scaled[rs, :] = value
        w_t[rs, :] = ref[:, hits:]

        @pl.when(half[0] == 0)
        def _():
            sa[rs, :] = value[:, :rows]

        @pl.when(half[0] == 1)
        def _():
            sa[rs, :] = value[:, rows:]

    full = jnp.transpose(w_t[...].astype(F32))
    w[...] = full.astype(BF16)
    triple = jnp.concatenate([ws_t[...].astype(F32)] * 3 + [jnp.zeros(ws_t.shape, F32)], 0)
    sides = jnp.transpose(triple)

    @pl.when(half[0] == 0)
    def _():
        w_turned[...] = full.astype(BF16)
        ws_turned[...] = sides.astype(BF16)

    @pl.when(half[0] == 1)
    def _():
        w_turned[...] = jnp.concatenate([full[width:], full[:width]], 0).astype(BF16)
        ws_turned[...] = jnp.concatenate([sides[width:], sides[:width]], 0).astype(BF16)


def last_body(
    near_dist, near_mix, mb, sb, w_t, ws_t, ah, ac, ma, live, w_turned, ws_turned,
    own, other, mine, theirs, dist_sc, mix_sc, mom_sc, oh, oc,
):
    window_terms(
        near_dist, near_mix, mb, sb, w_t, ws_t, dist_sc, mix_sc, mom_sc, oh, oc, (ah, ac)
    )
    width = mine.shape[0]
    hidden_grad = (oh[...]).astype(BF16)
    sums = jnp.transpose(oc[...])
    coords = lax.dot_general(ws_t[...], ma[...], NT, preferred_element_type=F32)
    pulled = sums[0:8] + sums[8:16] + sums[16:24]
    coord_grad = 2.0 * (pulled - coords * sums[4:5])
    row = lax.broadcasted_iota(jnp.int32, coord_grad.shape, 0)
    coord_grad = jnp.where(row < 4, coord_grad, 0.0)
    g1, g2, g3 = split3(coord_grad)
    parts = jnp.concatenate([g1, g2, g3, jnp.zeros_like(g1)], 0).astype(BF16)
    part_h = lax.dot_general(
        hidden_grad, ma[...], (((0,), (0,)), ((), ())), preferred_element_type=F32
    )
    triple = jnp.dot(parts, ma[...], preferred_element_type=F32)
    part_s = triple[0:8] + triple[8:16] + triple[16:24]
    own[:width, :] = part_h[:width]
    own[width:, :] = part_s
    other[:width, :] = part_h[width:]
    other[width:, :] = part_s
    grad = lax.dot_general(w_turned[...], hidden_grad, NT, preferred_element_type=F32)
    grad = grad + jnp.dot(ws_turned[...], parts, preferred_element_type=F32)
    grad = (grad * live[...]).astype(BF16)
    mine[...] = grad[:width]
    theirs[...] = grad[width:]


def call(body, operands, outs, cols, feats, extra=(), **kw):
    vmem = pl.BlockSpec(memory_space=pltpu.VMEM)
    return pl.pallas_call(
        body,
        out_shape=outs,
        in_specs=[vmem] * len(operands),
        out_specs=[vmem] * len(outs),
        scratch_shapes=[
            pltpu.VMEM((64, cols), BF16),
            pltpu.VMEM((2 * feats, cols), BF16),
            pltpu.VMEM((32, cols), BF16),
            *extra,
        ],
        compiler_params=pltpu.CompilerParams(vmem_limit_bytes=48 << 20),
        cost_estimate=pl.CostEstimate(
            flops=4 * cols * cols * feats, transcendentals=cols * cols // 2, bytes_accessed=4 * cols * feats
        ),
        **kw,
    )(*operands)


def local(inputs, weight_h, weight_s, cotangent, ranks, counts):
    block_total = lax.axis_size("blk")
    position = lax.axis_index("blk")
    my_half = lax.axis_index("feat")
    hits, width = cotangent.shape
    feats = 2 * width
    rows = hits // 2
    dims = weight_s.shape[1]
    blocks = jnp.arange(block_total, dtype=jnp.int32)
    spacing = (blocks - position) % block_total
    loop_gap = jnp.minimum(spacing, block_total - spacing)
    own_count = jnp.sum(jnp.where(blocks == position, counts, 0))
    window_count = jnp.sum(jnp.where(loop_gap <= WINDOW, counts, 0))
    live = (ranks < own_count).astype(F32)
    scale = 1.0 / jnp.sqrt(window_count.astype(F32))
    other_feat = lambda b, f: (b, 1 - f)

    vmem = pl.BlockSpec(memory_space=pltpu.VMEM)
    depth = inputs.shape[1]
    packed = pl.pallas_call(
        pack_body,
        out_shape=jax.ShapeDtypeStruct((width, hits + depth), BF16),
        in_specs=[vmem] * 2,
        out_specs=vmem,
    )(cotangent.T, weight_h.T)
    packed, inputs = lax.optimization_barrier((packed, inputs))
    arrived = moved(packed, other_feat)
    masked = inputs * live.astype(BF16)[:, None]
    partner = lambda b, f: (b ^ 1, f)

    def spread_out(x):
        steps = (partner, lambda b, f: (b - 2, f), lambda b, f: (b + 2, f))
        return [moved(x, step) for step in steps]

    def passed_on(after, before):
        return moved(jnp.where(position % 2 == 0, after, before), partner)

    masked_far = spread_out(masked)
    masked_far.append(passed_on(*masked_far[1:]))
    ws_t = jnp.zeros((8, depth), BF16).at[:dims].set(weight_s.T)
    shapes = [(feats, hits), (feats, rows), (depth, feats), (feats, depth), (depth, feats)]
    scaled, sa, w, w_t, w_turned, ws_turned = pl.pallas_call(
        spread_body,
        out_shape=[jax.ShapeDtypeStruct(shape, BF16) for shape in shapes + [(depth, 32)]],
        in_specs=[pl.BlockSpec(memory_space=pltpu.SMEM)] + [vmem] * 4,
        out_specs=[vmem] * 6,
        compiler_params=pltpu.CompilerParams(vmem_limit_bytes=32 << 20),
    )(my_half[None], packed, arrived, (live * scale)[None, :], ws_t)
    start = my_half * rows
    ma = lax.dynamic_slice_in_dim(masked, start, rows, 0)
    live_rows = lax.dynamic_slice_in_dim(live, start, rows, 0)[None, :]
    sums = [
        jax.ShapeDtypeStruct((rows, feats), F32),
        jax.ShapeDtypeStruct((rows, 32), F32),
    ]
    near = [
        jax.ShapeDtypeStruct((rows, 64), BF16),
        jax.ShapeDtypeStruct((rows, 2 * feats), BF16),
    ]
    scaled_far = spread_out(scaled)
    oh, oc, near_dist, near_mix = call(
        first_body, (ma, sa, masked, scaled, w, w_t, ws_t), sums + near, hits, feats
    )
    for i in range(3):
        oh, oc = call(
            next_body,
            (near_dist, near_mix, masked_far[i], scaled_far[i], w_t, ws_t, oh, oc),
            sums,
            hits,
            feats,
            input_output_aliases={6: 0, 7: 1},
        )
        if i == 0:
            oh, oc, *scaled_far[1:] = lax.optimization_barrier((oh, oc, *scaled_far[1:]))
            scaled_far.append(passed_on(*scaled_far[1:]))
    own, other, mine, theirs = call(
        last_body,
        (near_dist, near_mix, masked_far[-1], scaled_far[-1], w_t, ws_t, oh, oc)
        + (ma, live_rows, w_turned, ws_turned),
        [jax.ShapeDtypeStruct((width + 8, inputs.shape[1]), F32)] * 2
        + [jax.ShapeDtypeStruct((width, rows), BF16)] * 2,
        hits,
        feats,
        [pltpu.VMEM((rows, feats), F32), pltpu.VMEM((rows, 32), F32)],
    )
    total = own + moved(other, other_feat)
    step = 1
    while step < block_total:
        total = total + moved(total, lambda b, f, s=step: (b ^ s, f))
        step *= 2
    got = moved(theirs, other_feat)
    grad_inputs = jnp.where(
        my_half == 0, jnp.concatenate([mine, got], 1), jnp.concatenate([got, mine], 1)
    )
    return (grad_inputs.T, total[:width].T, total[width : width + dims].T)


def solution(mesh):
    placed = (P("blk", None), P(None, "feat"), P(), P("blk", "feat"), P("blk"), P())
    return jax.shard_map(
        local,
        mesh=mesh,
        in_specs=placed,
        out_specs=(P("blk", "feat"), P(None, "feat"), P()),
        check_vma=False,
    )
```

```python
import functools
import math

import jax
import jax.numpy as jnp
from jax import lax
from jax.experimental import pallas as pl
from jax.experimental.pallas import tpu as pltpu
from jax.sharding import PartitionSpec as P

WINDOW = 2
LOG2E = math.log2(math.e)
NT = (((1,), (1,)), ((), ()))
F32 = jnp.float32
BF16 = jnp.bfloat16
ROW_TILE = 512
COL_TILE = 1024


def moved(x, target):
    blks, feats = lax.axis_size("blk"), lax.axis_size("feat")
    route = []
    for b in range(blks):
        for f in range(feats):
            to_b, to_f = target(b, f)
            route.append((b * feats + f, (to_b % blks) * feats + to_f))
    return lax.ppermute(x, ("blk", "feat"), route)


def split3(v):
    high = v.astype(BF16).astype(F32)
    rest = v - high
    mid = rest.astype(BF16).astype(F32)
    return high, mid, rest - mid


def norm_rows(v, row, first):
    parts = split3(-LOG2E * jnp.sum(v * v, axis=0, keepdims=True))
    out = jnp.where(row < 6, 1.0, 0.0)
    for i, part in enumerate(parts):
        out = jnp.where(row == first + i, part, out)
    return out


def far_features(coords):
    row = lax.broadcasted_iota(jnp.int32, coords.shape, 0)
    b1, b2, b3 = split3(coords)
    zero = jnp.zeros_like(coords)
    dist = jnp.concatenate([b1, b2, b3, b1, b2, b1, norm_rows(coords, row, 3), zero], 0)
    moment = jnp.concatenate([jnp.where(row == 4, 1.0, b1), b2, b3, zero], 0)
    return dist.astype(BF16), moment.astype(BF16)


def near_features(coords):
    row = lax.broadcasted_iota(jnp.int32, coords.shape, 0)
    a1, a2, a3 = split3((2.0 * LOG2E) * coords)
    zero = jnp.zeros_like(coords)
    dist = jnp.concatenate([a1, a1, a1, a2, a2, a3, norm_rows(coords, row, 0), zero], 0)
    return jnp.transpose(dist).astype(BF16)


def window_terms(near_dist, near_mix, mb, sb, w_t, ws_t, dist_sc, mix_sc, mom_sc, oh, oc, acc):
    dist, moment = far_features(
        lax.dot_general(ws_t[...], mb[...], NT, preferred_element_type=F32)
    )
    dist_sc[...] = dist
    mom_sc[...] = moment
    half = mix_sc.shape[0] // 2
    mix_sc[:half, :] = lax.dot_general(
        w_t[...], mb[...], NT, preferred_element_type=F32
    ).astype(BF16)
    mix_sc[half:, :] = sb[...]
    rows, cols = near_dist.shape[0], mb.shape[0]
    for r in range(0, rows, ROW_TILE):
        rs = slice(r, r + ROW_TILE)
        total_h = total_c = None
        if acc is not None:
            total_h, total_c = acc[0][rs, :], acc[1][rs, :]
        for c in range(0, cols, COL_TILE):
            cs = slice(c, c + COL_TILE)
            power = jnp.dot(near_dist[rs, :], dist_sc[:, cs], preferred_element_type=F32)
            inner = jnp.dot(near_mix[rs, :], mix_sc[:, cs], preferred_element_type=F32)
            kernel = jnp.exp2(power)
            force = (kernel * inner).astype(BF16)
            part_h = lax.dot_general(
                kernel.astype(BF16), sb[:, cs], NT, preferred_element_type=F32
            )
            part_c = lax.dot_general(force, mom_sc[:, cs], NT, preferred_element_type=F32)
            total_h = part_h if total_h is None else total_h + part_h
            total_c = part_c if total_c is None else total_c + part_c
        oh[rs, :] = total_h
        oc[rs, :] = total_c


def first_body(ma, sa, mb, sb, w, w_t, ws_t, oh, oc, near_dist, near_mix, dist_sc, mix_sc, mom_sc):
    near_dist[...] = near_features(
        lax.dot_general(ws_t[...], ma[...], NT, preferred_element_type=F32)
    )
    half = near_mix.shape[1] // 2
    near_mix[:, :half] = jnp.transpose(sa[...].astype(F32)).astype(BF16)
    near_mix[:, half:] = jnp.dot(ma[...], w[...], preferred_element_type=F32).astype(BF16)
    window_terms(near_dist, near_mix, mb, sb, w_t, ws_t, dist_sc, mix_sc, mom_sc, oh, oc, None)


def next_body(near_dist, near_mix, mb, sb, w_t, ws_t, ah, ac, oh, oc, dist_sc, mix_sc, mom_sc):
    window_terms(
        near_dist, near_mix, mb, sb, w_t, ws_t, dist_sc, mix_sc, mom_sc, oh, oc, (ah, ac)
    )


def pack_body(cot_t, wh_t, out):
    hits = cot_t.shape[1]
    out[:, :hits] = cot_t[...]
    out[:, hits:] = wh_t[...]


def spread_body(half, packed, arrived, factor, ws_t, scaled, sa, w, w_t, w_turned, ws_turned):
    width = packed.shape[0]
    hits, rows = factor.shape[1], sa.shape[1]
    for i, ref in enumerate((packed, arrived)):
        rs = slice(i * width, (i + 1) * width)
        value = (ref[:, :hits].astype(F32) * factor[...]).astype(BF16)
        scaled[rs, :] = value
        w_t[rs, :] = ref[:, hits:]

        @pl.when(half[0] == 0)
        def _():
            sa[rs, :] = value[:, :rows]

        @pl.when(half[0] == 1)
        def _():
            sa[rs, :] = value[:, rows:]

    full = jnp.transpose(w_t[...].astype(F32))
    w[...] = full.astype(BF16)
    triple = jnp.concatenate([ws_t[...].astype(F32)] * 3 + [jnp.zeros(ws_t.shape, F32)], 0)
    sides = jnp.transpose(triple)

    @pl.when(half[0] == 0)
    def _():
        w_turned[...] = full.astype(BF16)
        ws_turned[...] = sides.astype(BF16)

    @pl.when(half[0] == 1)
    def _():
        w_turned[...] = jnp.concatenate([full[width:], full[:width]], 0).astype(BF16)
        ws_turned[...] = jnp.concatenate([sides[width:], sides[:width]], 0).astype(BF16)


def last_body(
    near_dist, near_mix, mb, sb, w_t, ws_t, ah, ac, ma, live, w_turned, ws_turned,
    pair, mine, theirs, dist_sc, mix_sc, mom_sc, oh, oc,
):
    window_terms(
        near_dist, near_mix, mb, sb, w_t, ws_t, dist_sc, mix_sc, mom_sc, oh, oc, (ah, ac)
    )
    width = mine.shape[0]
    hidden_grad = (oh[...]).astype(BF16)
    sums = jnp.transpose(oc[...])
    coords = lax.dot_general(ws_t[...], ma[...], NT, preferred_element_type=F32)
    pulled = sums[0:8] + sums[8:16] + sums[16:24]
    coord_grad = 2.0 * (pulled - coords * sums[4:5])
    row = lax.broadcasted_iota(jnp.int32, coord_grad.shape, 0)
    coord_grad = jnp.where(row < 4, coord_grad, 0.0)
    g1, g2, g3 = split3(coord_grad)
    parts = jnp.concatenate([g1, g2, g3, jnp.zeros_like(g1)], 0).astype(BF16)
    part_h = lax.dot_general(
        hidden_grad, ma[...], (((0,), (0,)), ((), ())), preferred_element_type=F32
    )
    triple = jnp.dot(parts, ma[...], preferred_element_type=F32)
    part_s = triple[0:8] + triple[8:16] + triple[16:24]
    for i in range(2):
        top = i * (width + 8)
        pair[top : top + width, :] = part_h[i * width : (i + 1) * width]
        pair[top + width : top + width + 8, :] = part_s
    grad = lax.dot_general(w_turned[...], hidden_grad, NT, preferred_element_type=F32)
    grad = grad + jnp.dot(ws_turned[...], parts, preferred_element_type=F32)
    grad = (grad * live[...]).astype(BF16)
    mine[...] = grad[:width]
    theirs[...] = grad[width:]


def call(body, operands, outs, cols, feats, extra=(), **kw):
    vmem = pl.BlockSpec(memory_space=pltpu.VMEM)
    return pl.pallas_call(
        body,
        out_shape=outs,
        in_specs=[vmem] * len(operands),
        out_specs=[vmem] * len(outs),
        scratch_shapes=[
            pltpu.VMEM((64, cols), BF16),
            pltpu.VMEM((2 * feats, cols), BF16),
            pltpu.VMEM((32, cols), BF16),
            *extra,
        ],
        compiler_params=pltpu.CompilerParams(vmem_limit_bytes=48 << 20),
        cost_estimate=pl.CostEstimate(
            flops=4 * cols * cols * feats, transcendentals=cols * cols // 2, bytes_accessed=4 * cols * feats
        ),
        **kw,
    )(*operands)


def local(inputs, weight_h, weight_s, cotangent, ranks, counts):
    block_total = lax.axis_size("blk")
    position = lax.axis_index("blk")
    my_half = lax.axis_index("feat")
    hits, width = cotangent.shape
    feats = 2 * width
    rows = hits // 2
    dims = weight_s.shape[1]
    blocks = jnp.arange(block_total, dtype=jnp.int32)
    spacing = (blocks - position) % block_total
    loop_gap = jnp.minimum(spacing, block_total - spacing)
    own_count = jnp.sum(jnp.where(blocks == position, counts, 0))
    window_count = jnp.sum(jnp.where(loop_gap <= WINDOW, counts, 0))
    live = (ranks < own_count).astype(F32)
    scale = 1.0 / jnp.sqrt(window_count.astype(F32))
    other_feat = lambda b, f: (b, 1 - f)

    vmem = pl.BlockSpec(memory_space=pltpu.VMEM)
    depth = inputs.shape[1]
    packed = pl.pallas_call(
        pack_body,
        out_shape=jax.ShapeDtypeStruct((width, hits + depth), BF16),
        in_specs=[vmem] * 2,
        out_specs=vmem,
    )(cotangent.T, weight_h.T)
    arrived = moved(packed, other_feat)
    masked = inputs * live.astype(BF16)[:, None]
    offsets = [1, -1, 2, -2][: 2 * WINDOW]
    masked_far = [moved(masked, lambda b, f, d=d: (b - d, f)) for d in offsets[:2]]
    ws_t = jnp.zeros((8, depth), BF16).at[:dims].set(weight_s.T)
    shapes = [(feats, hits), (feats, rows), (depth, feats), (feats, depth), (depth, feats)]
    scaled, sa, w, w_t, w_turned, ws_turned = pl.pallas_call(
        spread_body,
        out_shape=[jax.ShapeDtypeStruct(shape, BF16) for shape in shapes + [(depth, 32)]],
        in_specs=[pl.BlockSpec(memory_space=pltpu.SMEM)] + [vmem] * 4,
        out_specs=[vmem] * 6,
        compiler_params=pltpu.CompilerParams(vmem_limit_bytes=32 << 20),
    )(my_half[None], packed, arrived, (live * scale)[None, :], ws_t)
    start = my_half * rows
    ma = lax.dynamic_slice_in_dim(masked, start, rows, 0)
    live_rows = lax.dynamic_slice_in_dim(live, start, rows, 0)[None, :]
    sums = [
        jax.ShapeDtypeStruct((rows, feats), F32),
        jax.ShapeDtypeStruct((rows, 32), F32),
    ]
    near = [
        jax.ShapeDtypeStruct((rows, 64), BF16),
        jax.ShapeDtypeStruct((rows, 2 * feats), BF16),
    ]
    scaled_far = [moved(scaled, lambda b, f, d=d: (b - d, f)) for d in offsets[:2]]
    oh, oc, near_dist, near_mix = call(
        first_body, (ma, sa, masked, scaled, w, w_t, ws_t), sums + near, hits, feats
    )
    late_m, late_s, oh, oc = lax.optimization_barrier((masked, scaled, oh, oc))
    for d in offsets[2:]:
        masked_far.append(moved(late_m, lambda b, f, d=d: (b - d, f)))
        scaled_far.append(moved(late_s, lambda b, f, d=d: (b - d, f)))
    for mb, sb in list(zip(masked_far, scaled_far))[:-1]:
        oh, oc = call(
            next_body,
            (near_dist, near_mix, mb, sb, w_t, ws_t, oh, oc),
            sums,
            hits,
            feats,
            input_output_aliases={6: 0, 7: 1},
        )
    pair, mine, theirs = call(
        last_body,
        (near_dist, near_mix, masked_far[-1], scaled_far[-1], w_t, ws_t, oh, oc)
        + (ma, live_rows, w_turned, ws_turned),
        [jax.ShapeDtypeStruct((2 * (width + 8), inputs.shape[1]), F32)]
        + [jax.ShapeDtypeStruct((width, rows), BF16)] * 2,
        hits,
        feats,
        [pltpu.VMEM((rows, feats), F32), pltpu.VMEM((rows, 32), F32)],
    )
    far_half = block_total // 2
    swap = lambda mask: lambda b, f: (b ^ mask, f)
    pair = pair + moved(pair, swap(far_half))
    high = width + 8
    total = pair[:high] + moved(pair[high:], lambda b, f: (b ^ far_half, 1 - f))
    step = 1
    while step < far_half:
        mask = step | (step >> 1) if step in (4, 16) else step
        total = total + moved(total, swap(mask))
        step *= 2
    got = moved(theirs, other_feat)
    grad_inputs = jnp.where(
        my_half == 0, jnp.concatenate([mine, got], 1), jnp.concatenate([got, mine], 1)
    )
    return (grad_inputs.T, total[:width].T, total[width : width + dims].T)


def solution(mesh):
    placed = (P("blk", None), P(None, "feat"), P(), P("blk", "feat"), P("blk"), P())
    return jax.shard_map(
        local,
        mesh=mesh,
        in_specs=placed,
        out_specs=(P("blk", "feat"), P(None, "feat"), P()),
        check_vma=False,
    )
```

```python
import functools
import math

import jax
import jax.numpy as jnp
from jax import lax
from jax.experimental import pallas as pl
from jax.experimental.pallas import tpu as pltpu
from jax.sharding import PartitionSpec as P

WINDOW = 2
LOG2E = math.log2(math.e)
NT = (((1,), (1,)), ((), ()))
F32 = jnp.float32
BF16 = jnp.bfloat16
ROW_TILE = 1024
COL_TILE = 512


def moved(x, target):
    blks, feats = lax.axis_size("blk"), lax.axis_size("feat")
    route = []
    for b in range(blks):
        for f in range(feats):
            to_b, to_f = target(b, f)
            route.append((b * feats + f, (to_b % blks) * feats + to_f))
    return lax.ppermute(x, ("blk", "feat"), route)


def split3(v):
    high = v.astype(BF16).astype(F32)
    rest = v - high
    mid = rest.astype(BF16).astype(F32)
    return high, mid, rest - mid


def norm_rows(v, row, first):
    parts = split3(-LOG2E * jnp.sum(v * v, axis=0, keepdims=True))
    out = jnp.where(row < 6, 1.0, 0.0)
    for i, part in enumerate(parts):
        out = jnp.where(row == first + i, part, out)
    return out


def far_features(coords):
    row = lax.broadcasted_iota(jnp.int32, coords.shape, 0)
    b1, b2, b3 = split3(coords)
    zero = jnp.zeros_like(coords)
    dist = jnp.concatenate([b1, b2, b3, b1, b2, b1, norm_rows(coords, row, 3), zero], 0)
    moment = jnp.concatenate([jnp.where(row == 4, 1.0, b1), b2, b3, zero], 0)
    return dist.astype(BF16), moment.astype(BF16)


def near_features(coords):
    row = lax.broadcasted_iota(jnp.int32, coords.shape, 0)
    a1, a2, a3 = split3((2.0 * LOG2E) * coords)
    zero = jnp.zeros_like(coords)
    dist = jnp.concatenate([a1, a1, a1, a2, a2, a3, norm_rows(coords, row, 0), zero], 0)
    return jnp.transpose(dist).astype(BF16)


def window_terms(near_dist, near_mix, mb, sb, w_t, ws_t, dist_sc, mix_sc, mom_sc, oh, oc, acc):
    dist, moment = far_features(
        lax.dot_general(ws_t[...], mb[...], NT, preferred_element_type=F32)
    )
    dist_sc[...] = dist
    mom_sc[...] = moment
    half = mix_sc.shape[0] // 2
    mix_sc[:half, :] = lax.dot_general(
        w_t[...], mb[...], NT, preferred_element_type=F32
    ).astype(BF16)
    mix_sc[half:, :] = sb[...]
    rows, cols = near_dist.shape[0], mb.shape[0]
    for r in range(0, rows, ROW_TILE):
        rs = slice(r, r + ROW_TILE)
        total_h = total_c = None
        if acc is not None:
            total_h, total_c = acc[0][rs, :], acc[1][rs, :]
        for c in range(0, cols, COL_TILE):
            cs = slice(c, c + COL_TILE)
            power = jnp.dot(near_dist[rs, :], dist_sc[:, cs], preferred_element_type=F32)
            inner = jnp.dot(near_mix[rs, :], mix_sc[:, cs], preferred_element_type=F32)
            kernel = jnp.exp2(power)
            force = (kernel * inner).astype(BF16)
            part_h = lax.dot_general(
                kernel.astype(BF16), sb[:, cs], NT, preferred_element_type=F32
            )
            part_c = lax.dot_general(force, mom_sc[:, cs], NT, preferred_element_type=F32)
            total_h = part_h if total_h is None else total_h + part_h
            total_c = part_c if total_c is None else total_c + part_c
        oh[rs, :] = total_h
        oc[rs, :] = total_c


def first_body(ma, sa, mb, sb, w, w_t, ws_t, oh, oc, near_dist, near_mix, dist_sc, mix_sc, mom_sc):
    near_dist[...] = near_features(
        lax.dot_general(ws_t[...], ma[...], NT, preferred_element_type=F32)
    )
    half = near_mix.shape[1] // 2
    near_mix[:, :half] = jnp.transpose(sa[...].astype(F32)).astype(BF16)
    near_mix[:, half:] = jnp.dot(ma[...], w[...], preferred_element_type=F32).astype(BF16)
    window_terms(near_dist, near_mix, mb, sb, w_t, ws_t, dist_sc, mix_sc, mom_sc, oh, oc, None)


def next_body(near_dist, near_mix, mb, sb, w_t, ws_t, ah, ac, oh, oc, dist_sc, mix_sc, mom_sc):
    window_terms(
        near_dist, near_mix, mb, sb, w_t, ws_t, dist_sc, mix_sc, mom_sc, oh, oc, (ah, ac)
    )


def pack_body(cot_t, wh_t, out):
    hits = cot_t.shape[1]
    out[:, :hits] = cot_t[...]
    out[:, hits:] = wh_t[...]


def spread_body(half, packed, arrived, factor, ws_t, scaled, sa, w, w_t, w_turned, ws_turned):
    width = packed.shape[0]
    hits, rows = factor.shape[1], sa.shape[1]
    for i, ref in enumerate((packed, arrived)):
        rs = slice(i * width, (i + 1) * width)
        value = (ref[:, :hits].astype(F32) * factor[...]).astype(BF16)
        scaled[rs, :] = value
        w_t[rs, :] = ref[:, hits:]

        @pl.when(half[0] == 0)
        def _():
            sa[rs, :] = value[:, :rows]

        @pl.when(half[0] == 1)
        def _():
            sa[rs, :] = value[:, rows:]

    full = jnp.transpose(w_t[...].astype(F32))
    w[...] = full.astype(BF16)
    triple = jnp.concatenate([ws_t[...].astype(F32)] * 3 + [jnp.zeros(ws_t.shape, F32)], 0)
    sides = jnp.transpose(triple)

    @pl.when(half[0] == 0)
    def _():
        w_turned[...] = full.astype(BF16)
        ws_turned[...] = sides.astype(BF16)

    @pl.when(half[0] == 1)
    def _():
        w_turned[...] = jnp.concatenate([full[width:], full[:width]], 0).astype(BF16)
        ws_turned[...] = jnp.concatenate([sides[width:], sides[:width]], 0).astype(BF16)


def last_body(
    near_dist, near_mix, mb, sb, w_t, ws_t, ah, ac, ma, live, w_turned, ws_turned,
    pair, mine, theirs, dist_sc, mix_sc, mom_sc, oh, oc,
):
    window_terms(
        near_dist, near_mix, mb, sb, w_t, ws_t, dist_sc, mix_sc, mom_sc, oh, oc, (ah, ac)
    )
    width = mine.shape[0]
    hidden_grad = (oh[...]).astype(BF16)
    sums = jnp.transpose(oc[...])
    coords = lax.dot_general(ws_t[...], ma[...], NT, preferred_element_type=F32)
    pulled = sums[0:8] + sums[8:16] + sums[16:24]
    coord_grad = 2.0 * (pulled - coords * sums[4:5])
    row = lax.broadcasted_iota(jnp.int32, coord_grad.shape, 0)
    coord_grad = jnp.where(row < 4, coord_grad, 0.0)
    g1, g2, g3 = split3(coord_grad)
    parts = jnp.concatenate([g1, g2, g3, jnp.zeros_like(g1)], 0).astype(BF16)
    part_h = lax.dot_general(
        hidden_grad, ma[...], (((0,), (0,)), ((), ())), preferred_element_type=F32
    )
    triple = jnp.dot(parts, ma[...], preferred_element_type=F32)
    part_s = triple[0:8] + triple[8:16] + triple[16:24]
    for i in range(2):
        top = i * (width + 8)
        pair[top : top + width, :] = part_h[i * width : (i + 1) * width]
        pair[top + width : top + width + 8, :] = part_s
    grad = lax.dot_general(w_turned[...], hidden_grad, NT, preferred_element_type=F32)
    grad = grad + jnp.dot(ws_turned[...], parts, preferred_element_type=F32)
    grad = (grad * live[...]).astype(BF16)
    mine[...] = grad[:width]
    theirs[...] = grad[width:]


def call(body, operands, outs, cols, feats, extra=(), **kw):
    vmem = pl.BlockSpec(memory_space=pltpu.VMEM)
    return pl.pallas_call(
        body,
        out_shape=outs,
        in_specs=[vmem] * len(operands),
        out_specs=[vmem] * len(outs),
        scratch_shapes=[
            pltpu.VMEM((64, cols), BF16),
            pltpu.VMEM((2 * feats, cols), BF16),
            pltpu.VMEM((32, cols), BF16),
            *extra,
        ],
        compiler_params=pltpu.CompilerParams(vmem_limit_bytes=48 << 20),
        cost_estimate=pl.CostEstimate(
            flops=4 * cols * cols * feats, transcendentals=cols * cols // 2, bytes_accessed=4 * cols * feats
        ),
        **kw,
    )(*operands)


def local(inputs, weight_h, weight_s, cotangent, ranks, counts):
    block_total = lax.axis_size("blk")
    position = lax.axis_index("blk")
    my_half = lax.axis_index("feat")
    hits, width = cotangent.shape
    feats = 2 * width
    rows = hits // 2
    dims = weight_s.shape[1]
    blocks = jnp.arange(block_total, dtype=jnp.int32)
    spacing = (blocks - position) % block_total
    loop_gap = jnp.minimum(spacing, block_total - spacing)
    own_count = jnp.sum(jnp.where(blocks == position, counts, 0))
    window_count = jnp.sum(jnp.where(loop_gap <= WINDOW, counts, 0))
    live = (ranks < own_count).astype(F32)
    scale = 1.0 / jnp.sqrt(window_count.astype(F32))
    other_feat = lambda b, f: (b, 1 - f)

    vmem = pl.BlockSpec(memory_space=pltpu.VMEM)
    depth = inputs.shape[1]
    packed = pl.pallas_call(
        pack_body,
        out_shape=jax.ShapeDtypeStruct((width, hits + depth), BF16),
        in_specs=[vmem] * 2,
        out_specs=vmem,
    )(cotangent.T, weight_h.T)
    arrived = moved(packed, other_feat)
    masked = inputs * live.astype(BF16)[:, None]
    offsets = [1, -1, 2, -2][: 2 * WINDOW]
    masked_far = [moved(masked, lambda b, f, d=d: (b - d, f)) for d in offsets[:2]]
    ws_t = jnp.zeros((8, depth), BF16).at[:dims].set(weight_s.T)
    shapes = [(feats, hits), (feats, rows), (depth, feats), (feats, depth), (depth, feats)]
    scaled, sa, w, w_t, w_turned, ws_turned = pl.pallas_call(
        spread_body,
        out_shape=[jax.ShapeDtypeStruct(shape, BF16) for shape in shapes + [(depth, 32)]],
        in_specs=[pl.BlockSpec(memory_space=pltpu.SMEM)] + [vmem] * 4,
        out_specs=[vmem] * 6,
        compiler_params=pltpu.CompilerParams(vmem_limit_bytes=32 << 20),
    )(my_half[None], packed, arrived, (live * scale)[None, :], ws_t)
    start = my_half * rows
    ma = lax.dynamic_slice_in_dim(masked, start, rows, 0)
    live_rows = lax.dynamic_slice_in_dim(live, start, rows, 0)[None, :]
    sums = [
        jax.ShapeDtypeStruct((rows, feats), F32),
        jax.ShapeDtypeStruct((rows, 32), F32),
    ]
    near = [
        jax.ShapeDtypeStruct((rows, 64), BF16),
        jax.ShapeDtypeStruct((rows, 2 * feats), BF16),
    ]
    scaled_far = [moved(scaled, lambda b, f, d=d: (b - d, f)) for d in offsets[:2]]
    oh, oc, near_dist, near_mix = call(
        first_body, (ma, sa, masked, scaled, w, w_t, ws_t), sums + near, hits, feats
    )
    late_m, late_s, oh, oc = lax.optimization_barrier((masked, scaled, oh, oc))
    for d in offsets[2:]:
        masked_far.append(moved(late_m, lambda b, f, d=d: (b - d, f)))
        scaled_far.append(moved(late_s, lambda b, f, d=d: (b - d, f)))
    for mb, sb in list(zip(masked_far, scaled_far))[:-1]:
        oh, oc = call(
            next_body,
            (near_dist, near_mix, mb, sb, w_t, ws_t, oh, oc),
            sums,
            hits,
            feats,
            input_output_aliases={6: 0, 7: 1},
        )
    pair, mine, theirs = call(
        last_body,
        (near_dist, near_mix, masked_far[-1], scaled_far[-1], w_t, ws_t, oh, oc)
        + (ma, live_rows, w_turned, ws_turned),
        [jax.ShapeDtypeStruct((2 * (width + 8), inputs.shape[1]), F32)]
        + [jax.ShapeDtypeStruct((width, rows), BF16)] * 2,
        hits,
        feats,
        [pltpu.VMEM((rows, feats), F32), pltpu.VMEM((rows, 32), F32)],
    )
    far_half = block_total // 2
    swap = lambda mask: lambda b, f: (b ^ mask, f)
    pair = pair + moved(pair, swap(far_half))
    high = width + 8
    total = pair[:high] + moved(pair[high:], lambda b, f: (b ^ far_half, 1 - f))
    step = 1
    while step < far_half:
        mask = step | (step >> 1) if step in (4, 16) else step
        total = total + moved(total, swap(mask))
        step *= 2
    got = moved(theirs, other_feat)
    grad_inputs = jnp.where(
        my_half == 0, jnp.concatenate([mine, got], 1), jnp.concatenate([got, mine], 1)
    )
    return (grad_inputs.T, total[:width].T, total[width : width + dims].T)


def solution(mesh):
    placed = (P("blk", None), P(None, "feat"), P(), P("blk", "feat"), P("blk"), P())
    return jax.shard_map(
        local,
        mesh=mesh,
        in_specs=placed,
        out_specs=(P("blk", "feat"), P(None, "feat"), P()),
        check_vma=False,
    )
```

```python
import functools
import math

import jax
import jax.numpy as jnp
from jax import lax
from jax.experimental import pallas as pl
from jax.experimental.pallas import tpu as pltpu
from jax.sharding import PartitionSpec as P

WINDOW = 2
LOG2E = math.log2(math.e)
NT = (((1,), (1,)), ((), ()))
F32 = jnp.float32
BF16 = jnp.bfloat16
ROW_TILE = 1024
COL_TILE = 1024


def moved(x, target):
    blks, feats = lax.axis_size("blk"), lax.axis_size("feat")
    route = []
    for b in range(blks):
        for f in range(feats):
            to_b, to_f = target(b, f)
            route.append((b * feats + f, (to_b % blks) * feats + to_f))
    return lax.ppermute(x, ("blk", "feat"), route)


def split3(v):
    high = v.astype(BF16).astype(F32)
    rest = v - high
    mid = rest.astype(BF16).astype(F32)
    return high, mid, rest - mid


def norm_rows(v, row, first):
    parts = split3(-LOG2E * jnp.sum(v * v, axis=0, keepdims=True))
    out = jnp.where(row < 6, 1.0, 0.0)
    for i, part in enumerate(parts):
        out = jnp.where(row == first + i, part, out)
    return out


def far_features(coords):
    row = lax.broadcasted_iota(jnp.int32, coords.shape, 0)
    b1, b2, b3 = split3(coords)
    zero = jnp.zeros_like(coords)
    dist = jnp.concatenate([b1, b2, b3, b1, b2, b1, norm_rows(coords, row, 3), zero], 0)
    moment = jnp.concatenate([jnp.where(row == 4, 1.0, b1), b2, b3, zero], 0)
    return dist.astype(BF16), moment.astype(BF16)


def near_features(coords):
    row = lax.broadcasted_iota(jnp.int32, coords.shape, 0)
    a1, a2, a3 = split3((2.0 * LOG2E) * coords)
    zero = jnp.zeros_like(coords)
    dist = jnp.concatenate([a1, a1, a1, a2, a2, a3, norm_rows(coords, row, 0), zero], 0)
    return jnp.transpose(dist).astype(BF16)


def window_terms(near_dist, near_mix, mb, sb, w_t, ws_t, dist_sc, mix_sc, mom_sc, oh, oc, acc):
    dist, moment = far_features(
        lax.dot_general(ws_t[...], mb[...], NT, preferred_element_type=F32)
    )
    dist_sc[...] = dist
    mom_sc[...] = moment
    half = mix_sc.shape[0] // 2
    mix_sc[:half, :] = lax.dot_general(
        w_t[...], mb[...], NT, preferred_element_type=F32
    ).astype(BF16)
    mix_sc[half:, :] = sb[...]
    rows, cols = near_dist.shape[0], mb.shape[0]
    for r in range(0, rows, ROW_TILE):
        rs = slice(r, r + ROW_TILE)
        total_h = total_c = None
        if acc is not None:
            total_h, total_c = acc[0][rs, :], acc[1][rs, :]
        for c in range(0, cols, COL_TILE):
            cs = slice(c, c + COL_TILE)
            power = jnp.dot(near_dist[rs, :], dist_sc[:, cs], preferred_element_type=F32)
            inner = jnp.dot(near_mix[rs, :], mix_sc[:, cs], preferred_element_type=F32)
            kernel = jnp.exp2(power)
            force = (kernel * inner).astype(BF16)
            part_h = lax.dot_general(
                kernel.astype(BF16), sb[:, cs], NT, preferred_element_type=F32
            )
            part_c = lax.dot_general(force, mom_sc[:, cs], NT, preferred_element_type=F32)
            total_h = part_h if total_h is None else total_h + part_h
            total_c = part_c if total_c is None else total_c + part_c
        oh[rs, :] = total_h
        oc[rs, :] = total_c


def first_body(ma, sa, mb, sb, w, w_t, ws_t, oh, oc, near_dist, near_mix, dist_sc, mix_sc, mom_sc):
    near_dist[...] = near_features(
        lax.dot_general(ws_t[...], ma[...], NT, preferred_element_type=F32)
    )
    half = near_mix.shape[1] // 2
    near_mix[:, :half] = jnp.transpose(sa[...].astype(F32)).astype(BF16)
    near_mix[:, half:] = jnp.dot(ma[...], w[...], preferred_element_type=F32).astype(BF16)
    window_terms(near_dist, near_mix, mb, sb, w_t, ws_t, dist_sc, mix_sc, mom_sc, oh, oc, None)


def next_body(near_dist, near_mix, mb, sb, w_t, ws_t, ah, ac, oh, oc, dist_sc, mix_sc, mom_sc):
    window_terms(
        near_dist, near_mix, mb, sb, w_t, ws_t, dist_sc, mix_sc, mom_sc, oh, oc, (ah, ac)
    )


def pack_body(cot_t, wh_t, out):
    hits = cot_t.shape[1]
    out[:, :hits] = cot_t[...]
    out[:, hits:] = wh_t[...]


def spread_body(half, packed, arrived, factor, ws_t, scaled, sa, w, w_t, w_turned, ws_turned):
    width = packed.shape[0]
    hits, rows = factor.shape[1], sa.shape[1]
    for i, ref in enumerate((packed, arrived)):
        rs = slice(i * width, (i + 1) * width)
        value = (ref[:, :hits].astype(F32) * factor[...]).astype(BF16)
        scaled[rs, :] = value
        w_t[rs, :] = ref[:, hits:]

        @pl.when(half[0] == 0)
        def _():
            sa[rs, :] = value[:, :rows]

        @pl.when(half[0] == 1)
        def _():
            sa[rs, :] = value[:, rows:]

    full = jnp.transpose(w_t[...].astype(F32))
    w[...] = full.astype(BF16)
    triple = jnp.concatenate([ws_t[...].astype(F32)] * 3 + [jnp.zeros(ws_t.shape, F32)], 0)
    sides = jnp.transpose(triple)

    @pl.when(half[0] == 0)
    def _():
        w_turned[...] = full.astype(BF16)
        ws_turned[...] = sides.astype(BF16)

    @pl.when(half[0] == 1)
    def _():
        w_turned[...] = jnp.concatenate([full[width:], full[:width]], 0).astype(BF16)
        ws_turned[...] = jnp.concatenate([sides[width:], sides[:width]], 0).astype(BF16)


def last_body(
    near_dist, near_mix, mb, sb, w_t, ws_t, ah, ac, ma, live, w_turned, ws_turned,
    pair, mine, theirs, dist_sc, mix_sc, mom_sc, oh, oc,
):
    window_terms(
        near_dist, near_mix, mb, sb, w_t, ws_t, dist_sc, mix_sc, mom_sc, oh, oc, (ah, ac)
    )
    width = mine.shape[0]
    hidden_grad = (oh[...]).astype(BF16)
    sums = jnp.transpose(oc[...])
    coords = lax.dot_general(ws_t[...], ma[...], NT, preferred_element_type=F32)
    pulled = sums[0:8] + sums[8:16] + sums[16:24]
    coord_grad = 2.0 * (pulled - coords * sums[4:5])
    row = lax.broadcasted_iota(jnp.int32, coord_grad.shape, 0)
    coord_grad = jnp.where(row < 4, coord_grad, 0.0)
    g1, g2, g3 = split3(coord_grad)
    parts = jnp.concatenate([g1, g2, g3, jnp.zeros_like(g1)], 0).astype(BF16)
    part_h = lax.dot_general(
        hidden_grad, ma[...], (((0,), (0,)), ((), ())), preferred_element_type=F32
    )
    triple = jnp.dot(parts, ma[...], preferred_element_type=F32)
    part_s = triple[0:8] + triple[8:16] + triple[16:24]
    for i in range(2):
        top = i * (width + 8)
        pair[top : top + width, :] = part_h[i * width : (i + 1) * width]
        pair[top + width : top + width + 8, :] = part_s
    grad = lax.dot_general(w_turned[...], hidden_grad, NT, preferred_element_type=F32)
    grad = grad + jnp.dot(ws_turned[...], parts, preferred_element_type=F32)
    grad = (grad * live[...]).astype(BF16)
    mine[...] = grad[:width]
    theirs[...] = grad[width:]


def call(body, operands, outs, cols, feats, extra=(), **kw):
    vmem = pl.BlockSpec(memory_space=pltpu.VMEM)
    return pl.pallas_call(
        body,
        out_shape=outs,
        in_specs=[vmem] * len(operands),
        out_specs=[vmem] * len(outs),
        scratch_shapes=[
            pltpu.VMEM((64, cols), BF16),
            pltpu.VMEM((2 * feats, cols), BF16),
            pltpu.VMEM((32, cols), BF16),
            *extra,
        ],
        compiler_params=pltpu.CompilerParams(vmem_limit_bytes=48 << 20),
        cost_estimate=pl.CostEstimate(
            flops=4 * cols * cols * feats, transcendentals=cols * cols // 2, bytes_accessed=4 * cols * feats
        ),
        **kw,
    )(*operands)


def local(inputs, weight_h, weight_s, cotangent, ranks, counts):
    block_total = lax.axis_size("blk")
    position = lax.axis_index("blk")
    my_half = lax.axis_index("feat")
    hits, width = cotangent.shape
    feats = 2 * width
    rows = hits // 2
    dims = weight_s.shape[1]
    blocks = jnp.arange(block_total, dtype=jnp.int32)
    spacing = (blocks - position) % block_total
    loop_gap = jnp.minimum(spacing, block_total - spacing)
    own_count = jnp.sum(jnp.where(blocks == position, counts, 0))
    window_count = jnp.sum(jnp.where(loop_gap <= WINDOW, counts, 0))
    live = (ranks < own_count).astype(F32)
    scale = 1.0 / jnp.sqrt(window_count.astype(F32))
    other_feat = lambda b, f: (b, 1 - f)

    vmem = pl.BlockSpec(memory_space=pltpu.VMEM)
    depth = inputs.shape[1]
    packed = pl.pallas_call(
        pack_body,
        out_shape=jax.ShapeDtypeStruct((width, hits + depth), BF16),
        in_specs=[vmem] * 2,
        out_specs=vmem,
    )(cotangent.T, weight_h.T)
    arrived = moved(packed, other_feat)
    masked = inputs * live.astype(BF16)[:, None]
    offsets = [1, -1, 2, -2][: 2 * WINDOW]
    masked_far = [moved(masked, lambda b, f, d=d: (b - d, f)) for d in offsets[:2]]
    ws_t = jnp.zeros((8, depth), BF16).at[:dims].set(weight_s.T)
    shapes = [(feats, hits), (feats, rows), (depth, feats), (feats, depth), (depth, feats)]
    scaled, sa, w, w_t, w_turned, ws_turned = pl.pallas_call(
        spread_body,
        out_shape=[jax.ShapeDtypeStruct(shape, BF16) for shape in shapes + [(depth, 32)]],
        in_specs=[pl.BlockSpec(memory_space=pltpu.SMEM)] + [vmem] * 4,
        out_specs=[vmem] * 6,
        compiler_params=pltpu.CompilerParams(vmem_limit_bytes=32 << 20),
    )(my_half[None], packed, arrived, (live * scale)[None, :], ws_t)
    start = my_half * rows
    ma = lax.dynamic_slice_in_dim(masked, start, rows, 0)
    live_rows = lax.dynamic_slice_in_dim(live, start, rows, 0)[None, :]
    sums = [
        jax.ShapeDtypeStruct((rows, feats), F32),
        jax.ShapeDtypeStruct((rows, 32), F32),
    ]
    near = [
        jax.ShapeDtypeStruct((rows, 64), BF16),
        jax.ShapeDtypeStruct((rows, 2 * feats), BF16),
    ]
    scaled_far = [moved(scaled, lambda b, f, d=d: (b - d, f)) for d in offsets[:2]]
    oh, oc, near_dist, near_mix = call(
        first_body, (ma, sa, masked, scaled, w, w_t, ws_t), sums + near, hits, feats
    )
    late_m, late_s, oh, oc = lax.optimization_barrier((masked, scaled, oh, oc))
    for d in offsets[2:]:
        masked_far.append(moved(late_m, lambda b, f, d=d: (b - d, f)))
        scaled_far.append(moved(late_s, lambda b, f, d=d: (b - d, f)))
    for mb, sb in list(zip(masked_far, scaled_far))[:-1]:
        oh, oc = call(
            next_body,
            (near_dist, near_mix, mb, sb, w_t, ws_t, oh, oc),
            sums,
            hits,
            feats,
            input_output_aliases={6: 0, 7: 1},
        )
    pair, mine, theirs = call(
        last_body,
        (near_dist, near_mix, masked_far[-1], scaled_far[-1], w_t, ws_t, oh, oc)
        + (ma, live_rows, w_turned, ws_turned),
        [jax.ShapeDtypeStruct((2 * (width + 8), inputs.shape[1]), F32)]
        + [jax.ShapeDtypeStruct((width, rows), BF16)] * 2,
        hits,
        feats,
        [pltpu.VMEM((rows, feats), F32), pltpu.VMEM((rows, 32), F32)],
    )
    far_half = block_total // 2
    swap = lambda mask: lambda b, f: (b ^ mask, f)
    pair = pair + moved(pair, swap(far_half))
    high = width + 8
    total = pair[:high] + moved(pair[high:], lambda b, f: (b ^ far_half, 1 - f))
    step = 1
    while step < far_half:
        mask = step | (step >> 1) if step in (4, 16) else step
        total = total + moved(total, swap(mask))
        step *= 2
    got = moved(theirs, other_feat)
    grad_inputs = jnp.where(
        my_half == 0, jnp.concatenate([mine, got], 1), jnp.concatenate([got, mine], 1)
    )
    return (grad_inputs.T, total[:width].T, total[width : width + dims].T)


def solution(mesh):
    placed = (P("blk", None), P(None, "feat"), P(), P("blk", "feat"), P("blk"), P())
    return jax.shard_map(
        local,
        mesh=mesh,
        in_specs=placed,
        out_specs=(P("blk", "feat"), P(None, "feat"), P()),
        check_vma=False,
    )
```
